128 devices in a mesh: prow: 32 (over x, z_lo, y), pcol: 4 (over z_hi, core).
Axes of the slice: x: 4, y: 4, z: 4 (z_hi: 2, z_lo: 2; z = z_hi * 2 + z_lo), core: 2. Of those that a mesh axis runs over, the one named last changes fastest.
Arguments:
- inverse_band: float32 [4096, 4096], P('prow', 'pcol'), may hold values from -0.09375 to 0.09375
- factor_panel: float32 [2, 4096, 512], P(None, 'prow', 'pcol'), may hold values from -0.6 to 0.6
- diag_inverse: float32 [2, 512, 512], replicated, may hold values from -1 to 2, as said below
- ancestors: int32 [2, 63], replicated, may hold values from 0 to 63, as said below
- counts: int32 [2], replicated, may hold values from 1 to 63, as said below
Outputs:
- new_column: float32 [2, 4096, 512], P(None, 'prow', 'pcol')
- diag_block: float32 [2, 512, 512], P(None, 'prow', 'pcol')
The draws below stay inside these ranges and needn't reach their ends.
Inputs may be any that keep to these rules, and one draw needn't show every extreme that they name: Each row holds distinct block numbers; its first counts[s] entries are in increasing order and include 63; the entries after them are other block numbers, which are not ancestors. One of the two counts is 63; the other is below 63. `diag_inverse`: lower triangular; diagonal entries from 0.5 to 2.
All inputs are finite; a program needn't handle non-finite values.
Results may differ from the reference program's by a relative error of at most 0.000073.
Values sent between devices are 32-bit elements; how exact they have to be, the bound alone decides.
No kernel may reach another device: no remote copies, remote signals or barrier semaphores. Data moves between devices by JAX's collectives and lax.ppermute only.
A program may use at most 64 MiB of HBM per device.

```python
import jax
import jax.numpy as jnp
from jax import lax

W = 512
BS = 64
BLK_DEV = 2
NBLK = 64
MAXA = 63
N_PROW = 32
N_PCOL = 4


def ancestor_lists(key):
    full_key = jax.random.fold_in(key, 17)
    length_key = jax.random.fold_in(key, 13)
    full_one = jax.random.randint(full_key, (), 0, 2).astype(jnp.int32)
    other_length = jax.random.randint(length_key, (), 1, MAXA).astype(jnp.int32)
    which = jnp.arange(2, dtype=jnp.int32)
    lengths = jnp.where(which == full_one, jnp.int32(MAXA), other_length).astype(jnp.int32)
    blocks = jnp.arange(NBLK, dtype=jnp.int32)
    picked_lists = []
    for supernode in range(2):
        score_key = jax.random.fold_in(key, 23 + supernode)
        scores = jax.random.randint(score_key, (NBLK,), 0, 4 * NBLK).astype(jnp.int32) + 2 * blocks
        scores = jnp.where(blocks == NBLK - 1, 8 * NBLK, scores)
        distinct = scores * NBLK + blocks
        ordering = jnp.argsort(-distinct)
        ranking = jnp.argsort(ordering)
        chosen = ranking < lengths[supernode]
        sort_keys = jnp.where(chosen, blocks, NBLK + blocks).astype(jnp.int32)
        placed = jnp.sort(sort_keys)[:MAXA]
        picked = jnp.where(placed >= NBLK, placed - NBLK, placed)
        picked_lists.append(picked.astype(jnp.int32))
    return (jnp.stack(picked_lists).astype(jnp.int32), lengths)


def draw_ancestors(key, part):
    listed, lengths = ancestor_lists(jax.random.fold_in(key, 5))
    return listed


def draw_counts(key, part):
    listed, lengths = ancestor_lists(jax.random.fold_in(key, 5))
    return lengths


def draw_diag_inverse(key, part):
    subkeys = jax.random.split(key, 2)
    diagonal = jnp.exp(jax.random.uniform(subkeys[0], (2, W), jnp.float32, -0.6931, 0.6931))
    below_diag = jax.random.uniform(subkeys[1], (2, W, W), jnp.float32, -1.0, 1.0) * (3.0 / W) ** 0.5
    triangle = jnp.tril(below_diag, -1) + diagonal[:, :, None] * jnp.eye(W, dtype=jnp.float32)[None, :, :]
    return triangle.astype(jnp.float32)


def level_of(key, extent, cuts, least, top_value):
    def one(dim, parts):
        draws = jax.random.uniform(jax.random.fold_in(jax.random.fold_in(key, 6), dim), (parts,), jnp.float32, least / len(cuts), top_value / len(cuts))
        return jnp.repeat(jnp.exp(draws), extent[dim] // parts).reshape((-1,) + (1,) * (len(extent) - dim - 1))

    level = one(*cuts[0])
    for cut in cuts[1:]:
        level = level * one(*cut)
    return level


def noise(rng, extent, scale, bound, cuts=(), held_as=jnp.bfloat16):
    values = jax.random.normal(rng, extent, jnp.float32) * scale
    if len(cuts) > 0:
        values = level_of(rng, extent, cuts, -0.22, 0.18) * values
    return jnp.clip(values, min=-bound, max=bound).astype(held_as)


def setup_inputs(seed: int = 0) -> dict:
    splits = jax.random.split(jax.random.key(seed), 6)
    return {
        "inverse_band": noise(splits[0], (NBLK * BS, NBLK * BS), (MAXA * BS) ** -0.5, 0.09375, ((0, 32), (1, 4)), jnp.float32),
        "factor_panel": noise(splits[1], (2, NBLK * BS, W), 0.1, 0.6, ((1, 32), (2, 4)), jnp.float32),
        "diag_inverse": draw_diag_inverse(jax.random.fold_in(splits[5], 71), 0),
        "ancestors": draw_ancestors(jax.random.fold_in(splits[5], 71), 0),
        "counts": draw_counts(jax.random.fold_in(splits[5], 71), 0),
    }


precise = lax.Precision.HIGHEST


def reference(inverse_band, factor_panel, diag_inverse, ancestors, counts):
    slot_ids = jnp.arange(NBLK, dtype=jnp.int32)
    slot_block = (slot_ids % BLK_DEV) * N_PROW + slot_ids // BLK_DEV
    per_col = NBLK // N_PCOL
    col_group = slot_ids // per_col
    col_rest = slot_ids % per_col
    col_block = (col_rest % BLK_DEV) * N_PROW + (col_rest // BLK_DEV) * N_PCOL + col_group
    row_of_col = (col_block % N_PROW) * BLK_DEV + col_block // N_PROW
    filled = jnp.arange(MAXA, dtype=jnp.int32)[None, :] < counts[:, None]
    matches = (ancestors[:, :, None] == slot_block[None, None, :]) & filled[:, :, None]
    members = jnp.any(matches, axis=1).astype(jnp.float32)[:, :, None, None]
    scaled = jnp.einsum("srk,skw->srw", factor_panel, diag_inverse, precision=precise)
    scaled = scaled.reshape(2, NBLK, BS, W) * members
    arranged = scaled[:, row_of_col].reshape(2, NBLK * BS, W)
    applied = jnp.einsum("rc,scw->srw", inverse_band, arranged, precision=precise)
    applied = applied.reshape(2, NBLK, BS, W) * members
    new_column = -applied.reshape(2, NBLK * BS, W)
    flat_scaled = scaled.reshape(2, NBLK * BS, W)
    diag_block = jnp.einsum("skr,skw->srw", diag_inverse, diag_inverse, precision=precise)
    diag_block = diag_block - jnp.einsum("srk,srw->skw", flat_scaled, new_column, precision=precise)
    return new_column, diag_block
```

```python
import jax
import jax.numpy as jnp
from jax import lax
from jax.sharding import Mesh, PartitionSpec as P

W = 512
BS = 64
Q = 128
AXES = ("x", "zl", "y", "zh", "core")
SIZES = (4, 2, 4, 2, 2)
PROW = ("x", "zl", "y")
PCOL = ("zh", "core")

near = lax.Precision.HIGH
SWAP = [(0, 1), (1, 0)]


def moved(flip_zl):
    pairs = []
    for zl in range(2):
        for y in range(4):
            for c in range(4):
                to = 1 - zl if flip_zl else zl
                pairs.append(((zl * 4 + y) * 4 + c, (to * 4 + c) * 4 + y))
    return pairs


def pick(x, i, dim):
    return lax.dynamic_index_in_dim(x, i, dim, keepdims=False)


def local(band, panel, diag_inverse, ancestors, counts):
    zl = lax.axis_index("zl")
    zh = lax.axis_index("zh")
    core = lax.axis_index("core")
    prow = lax.axis_index(PROW)
    pcol = lax.axis_index(PCOL)
    block_ids = jnp.arange(2, dtype=jnp.int32) * 32 + prow
    filled = jnp.arange(ancestors.shape[1], dtype=jnp.int32)[None, :] < counts[:, None]
    matches = (ancestors[:, :, None] == block_ids[None, None, :]) & filled[:, :, None]
    members = jnp.any(matches, axis=1).astype(jnp.float32)
    row_mask = jnp.repeat(members, BS, axis=1)[:, :, None]
    masked = panel * row_mask
    mine = pick(masked, zl, 0)
    other = pick(masked, 1 - zl, 0)
    got_mine = lax.ppermute(mine, ("zl", "y", "zh", "core"), moved(False))
    got_other = lax.ppermute(other, ("zl", "y", "zh", "core"), moved(True))
    band_other = lax.ppermute(band, "zl", SWAP)
    rows_other = lax.ppermute(other, "zl", SWAP)
    rows = jnp.stack([mine, rows_other])
    rows_core = lax.ppermute(rows, "core", SWAP)
    low = jnp.where(core == 0, rows, rows_core)
    high = jnp.where(core == 0, rows_core, rows)
    half = jnp.concatenate([low, high], axis=2)
    half_far = lax.ppermute(half, "zh", SWAP)
    full = jnp.concatenate(
        [jnp.where(zh == 0, half, half_far), jnp.where(zh == 0, half_far, half)], axis=2
    ).reshape(2 * Q, W)
    diag_mine = pick(diag_inverse, zl, 0)
    scaled = jnp.dot(full, diag_mine, precision=near)

    block = jnp.concatenate(
        [jnp.where(zl == 0, got_mine, got_other), jnp.where(zl == 0, got_other, got_mine)], axis=0
    )
    spread = jnp.broadcast_to(block[None], (16, 2 * Q, Q))
    gathered = lax.all_to_all(spread, ("x", "y"), 0, 0, tiled=True)
    stacked = gathered.reshape(4, 4, 2 * Q, Q).transpose(0, 2, 1, 3).reshape(8 * Q, W)
    both = jnp.concatenate([band, band_other], axis=0)
    product = jnp.dot(both, stacked, precision=near)
    partial = jnp.dot(product, diag_mine, precision=near)

    corr = lax.dot_general(scaled, partial, (((0,), (0,)), ((), ())), precision=near)
    corr = corr.reshape(W, 2, 2, Q)
    corr_sum = pick(corr, core, 2) + lax.ppermute(pick(corr, 1 - core, 2), "core", SWAP)
    corr_sum = corr_sum.reshape(32, 16, 2, Q).transpose(0, 2, 1, 3).reshape(64, 16, Q)

    parts = partial.reshape(2, Q, 2, 2, Q)
    kept = pick(parts, core, 3) + lax.ppermute(pick(parts, 1 - core, 3), "core", SWAP)
    near_part = pick(kept, zh, 2)
    far_part = pick(kept, 1 - zh, 2)
    in_a = lax.ppermute(far_part[0], "zh", SWAP)
    in_b = lax.ppermute(near_part[1], "zl", SWAP)
    in_c = lax.ppermute(far_part[1], ("zl", "zh"), [(0, 3), (1, 2), (2, 1), (3, 0)])
    own_sum = near_part[0] + in_a
    other_sum = in_b + in_c
    summed = jnp.stack(
        [jnp.where(zl == 0, own_sum, other_sum), jnp.where(zl == 0, other_sum, own_sum)]
    )
    new_column = -(summed * row_mask)

    landed = lax.all_to_all(corr_sum, ("x", "zl", "y", "zh"), 0, 0, tiled=True)
    reduced = landed.reshape(4, 2, 8, 16, Q).sum(axis=(0, 2))
    row_factor = lax.dynamic_slice_in_dim(diag_inverse, prow * 16, 16, 2)
    col_factor = lax.dynamic_slice_in_dim(diag_inverse, pcol * Q, Q, 2)
    square = jnp.einsum("skr,skw->srw", row_factor, col_factor, precision=near)
    return (new_column, square + reduced)


def solution(mesh):
    fine = Mesh(mesh.devices.reshape(SIZES), AXES)
    in_specs = (P(PROW, PCOL), P(None, PROW, PCOL), P(), P(), P())
    out_specs = (P(None, PROW, PCOL), P(None, PROW, PCOL))
    return jax.shard_map(local, mesh=fine, in_specs=in_specs, out_specs=out_specs, check_vma=False)
```

```python
import jax
import jax.numpy as jnp
import numpy as np
from jax import lax
from jax.experimental import pallas as pl
from jax.experimental.pallas import tpu as pltpu
from jax.sharding import Mesh, PartitionSpec as P

W = 512
BS = 64
Q = 128
AXES = ("x", "zl", "y", "zh", "core")
SIZES = (4, 2, 4, 2, 2)
PROW = ("x", "zl", "y")
PCOL = ("zh", "core")

near = lax.Precision.HIGH
SWAP = [(0, 1), (1, 0)]
EVEN = [(0, 1), (1, 0), (2, 3), (3, 2)]
ODD = [(0, 3), (3, 0), (1, 2), (2, 1)]
ALL_VMEM = pl.BlockSpec(memory_space=pltpu.VMEM)
ALL_SMEM = pl.BlockSpec(memory_space=pltpu.SMEM)


def route(where):
    pairs = []
    for source in np.ndindex(*SIZES):
        x, zl, y, zh, core = source
        target = where(x, zl, y, 2 * zh + core)
        tx, tzl, ty, tc = target
        pairs.append(
            (
                int(np.ravel_multi_index(source, SIZES)),
                int(np.ravel_multi_index((tx, tzl, ty, tc // 2, tc % 2), SIZES)),
            )
        )
    return pairs


def pick(x, i, dim):
    return lax.dynamic_index_in_dim(x, i, dim, keepdims=False)


def split(v):
    high = v.astype(jnp.bfloat16)
    return high, (v - high.astype(jnp.float32)).astype(jnp.bfloat16)


def dot3(left, right):
    ah, al = left
    bh, bl = right

    def one(a, b):
        return jnp.dot(a, b, preferred_element_type=jnp.float32)

    return one(ah, bh) + (one(ah, bl) + one(al, bh))


def kernel(
    where,
    band_own,
    band_other,
    col_mask,
    a1,
    a1r,
    a2,
    a2r,
    b1,
    b1r,
    b2,
    b2r,
    diag_mine,
    scaled_t,
    corr_keep,
    corr_send,
    part_keep,
    part_send,
    band_hi,
    band_lo,
    panel_hi,
    panel_lo,
    diag_hi,
    diag_lo,
):
    x = where[0]
    y = where[1]
    zl = where[2]
    zh = where[3]
    core = where[4]
    pieces = {}
    for ref, qs in ((a1, (0, 1)), (a1r, (3, 2))):
        for i, q in enumerate(qs):
            for j, xo in enumerate((0, 1)):
                pieces[0, xo, q] = (ref, i, j)
    for ref, qs in ((a2, (0, 3)), (a2r, (1, 2))):
        for i, q in enumerate(qs):
            for j, xo in enumerate((3, 2)):
                pieces[0, xo, q] = (ref, i, j)
    for ref, xs in ((b1, (0, 1)), (b1r, (3, 2))):
        for i, xo in enumerate(xs):
            for j, q in enumerate((0, 1)):
                pieces[1, xo, q] = (ref, i, j)
    for ref, xs in ((b2, (0, 3)), (b2r, (1, 2))):
        for i, xo in enumerate(xs):
            for j, q in enumerate((3, 2)):
                pieces[1, xo, q] = (ref, i, j)
    for (stream, xo, q), (ref, i, j) in pieces.items():
        hi, lo = split(ref[i, j])
        rows = slice((2 * xo + stream) * Q, (2 * xo + stream + 1) * Q)
        cols = slice(q * Q, (q + 1) * Q)
        panel_hi[rows, cols] = hi
        panel_lo[rows, cols] = lo
    for xo in range(4):
        for stream in range(2):
            side = zl if stream == 0 else 1 - zl
            start = pl.multiple_of((x ^ xo) * (2 * Q) + side * Q, Q)
            mask = col_mask[:, pl.ds(start, Q)]
            cols = slice((2 * xo + stream) * Q, (2 * xo + stream + 1) * Q)
            for r, ref in enumerate((band_own, band_other)):
                hi, lo = split(ref[:, pl.ds(start, Q)] * mask)
                band_hi[r * Q : (r + 1) * Q, cols] = hi
                band_lo[r * Q : (r + 1) * Q, cols] = lo
    for q in range(4):
        start = pl.multiple_of((y ^ q) * Q, Q)
        hi, lo = split(diag_mine[pl.ds(start, Q), :])
        diag_hi[q * Q : (q + 1) * Q, :] = hi
        diag_lo[q * Q : (q + 1) * Q, :] = lo
    product = dot3((band_hi[...], band_lo[...]), (panel_hi[...], panel_lo[...]))
    partial = dot3(split(product), (diag_hi[...], diag_lo[...]))
    corr = dot3(split(scaled_t[...]), split(partial))

    def emit(value, keep, send, own_zh):
        for c in range(2):

            @pl.when(core == c)
            def _():
                for h in range(2):
                    for ref, k in ((keep, c), (send, 1 - c)):
                        part = value[:, (2 * h + k) * Q : (2 * h + k + 1) * Q]
                        if own_zh:
                            side = jnp.where(zh == h, 0, 1)
                            ref[:, side] = part.reshape(2, Q, Q)
                        else:
                            ref[:, h] = part.reshape(32, 16, Q)

    emit(corr, corr_keep, corr_send, False)
    emit(partial, part_keep, part_send, True)


def local_work(where, *arrays):
    corr = jax.ShapeDtypeStruct((32, 2, 16, Q), jnp.float32)
    part = jax.ShapeDtypeStruct((2, 2, Q, Q), jnp.float32)
    return pl.pallas_call(
        kernel,
        out_shape=(corr, corr, part, part),
        in_specs=[ALL_SMEM] + [ALL_VMEM] * len(arrays),
        out_specs=(ALL_VMEM,) * 4,
        scratch_shapes=[
            pltpu.VMEM((2 * Q, 8 * Q), jnp.bfloat16),
            pltpu.VMEM((2 * Q, 8 * Q), jnp.bfloat16),
            pltpu.VMEM((8 * Q, W), jnp.bfloat16),
            pltpu.VMEM((8 * Q, W), jnp.bfloat16),
            pltpu.VMEM((W, W), jnp.bfloat16),
            pltpu.VMEM((W, W), jnp.bfloat16),
        ],
        compiler_params=pltpu.CompilerParams(vmem_limit_bytes=40 * 1024 * 1024),
    )(where, *arrays)


def local(band, panel, diag_inverse, ancestors, counts):
    x = lax.axis_index("x")
    y = lax.axis_index("y")
    zl = lax.axis_index("zl")
    zh = lax.axis_index("zh")
    core = lax.axis_index("core")
    prow = lax.axis_index(PROW)
    pcol = lax.axis_index(PCOL)
    mine = pick(panel, zl, 0)
    other = pick(panel, 1 - zl, 0)
    a_here = lax.ppermute(mine, AXES, route(lambda x, zl, y, c: (x, zl, c, y)))
    b_here = lax.ppermute(other, AXES, route(lambda x, zl, y, c: (x, 1 - zl, c, y)))
    a_next = lax.ppermute(mine, AXES, route(lambda x, zl, y, c: (x ^ 1, zl, c, y)))
    b_next = lax.ppermute(other, AXES, route(lambda x, zl, y, c: (x, 1 - zl, c ^ 1, y)))
    band_other = lax.ppermute(band, "zl", SWAP)

    def members_of(ids):
        filled = jnp.arange(ancestors.shape[1], dtype=jnp.int32)[None, :] < counts[:, None]
        matches = (ancestors[:, :, None] == ids[None, None, :]) & filled[:, :, None]
        return jnp.any(matches, axis=1).astype(jnp.float32)

    row_ids = jnp.arange(2, dtype=jnp.int32) * 32 + prow
    other_row = prow + 4 - 8 * zl
    other_ids = jnp.arange(2, dtype=jnp.int32) * 32 + other_row
    slots = jnp.arange(16, dtype=jnp.int32)
    col_ids = (slots % 2) * 32 + (slots // 2) * 4 + pcol
    members = members_of(jnp.concatenate([row_ids, other_ids, col_ids]))
    row_mask = jnp.repeat(members[:, :2], BS, axis=1)[:, :, None]
    pair_mask = jnp.repeat(pick(members, zl, 0)[:4], BS).reshape(2, Q, 1)
    col_mask = jnp.repeat(pick(members, zl, 0)[4:], BS)[None, :]

    a12 = jnp.stack([a_here, a_next])
    b12 = jnp.stack([b_here, b_next])
    a34 = lax.ppermute(a12, "x", ODD)
    b34 = lax.ppermute(b12, "y", ODD)
    a1 = jnp.stack([a12, lax.ppermute(a12, "y", EVEN)])
    b1 = jnp.stack([b12, lax.ppermute(b12, "x", EVEN)])
    a2 = jnp.stack([a34, lax.ppermute(a34, "y", ODD)])
    b2 = jnp.stack([b34, lax.ppermute(b34, "x", ODD)])
    a1r = lax.ppermute(a1, "y", ODD)
    b1r = lax.ppermute(b1, "x", ODD)
    a2r = lax.ppermute(a2, "y", EVEN)
    b2r = lax.ppermute(b2, "x", EVEN)

    rows = jnp.stack([mine, lax.ppermute(other, "zl", SWAP)]) * pair_mask
    rows_core = lax.ppermute(rows, "core", SWAP)
    half = jnp.concatenate(
        [jnp.where(core == 0, rows, rows_core), jnp.where(core == 0, rows_core, rows)], axis=2
    )
    half_far = lax.ppermute(half, "zh", SWAP)
    full = jnp.concatenate(
        [jnp.where(zh == 0, half, half_far), jnp.where(zh == 0, half_far, half)], axis=2
    ).reshape(2 * Q, W)
    diag_mine = pick(diag_inverse, zl, 0)
    scaled_t = lax.dot_general(diag_mine, full, (((0,), (1,)), ((), ())), precision=near)
    row_factor = lax.dynamic_slice_in_dim(diag_inverse, prow * 16, 16, 2)
    col_factor = lax.dynamic_slice_in_dim(diag_inverse, pcol * Q, Q, 2)
    square = jnp.einsum("skr,skw->srw", row_factor, col_factor, precision=near)
    scaled_t, square = lax.optimization_barrier((scaled_t, square))

    where = jnp.stack([x, y, zl, zh, core]).astype(jnp.int32)
    corr_keep, corr_send, part_keep, part_send = local_work(
        where, band, band_other, col_mask, a1, a1r, a2, a2r, b1, b1r, b2, b2r, diag_mine, scaled_t
    )
    corr = corr_keep + lax.ppermute(corr_send, "core", SWAP)
    landed = lax.all_to_all(corr.reshape(64, 16, Q), ("x", "zl", "y", "zh"), 0, 0, tiled=True)
    parts = part_keep + lax.ppermute(part_send, "core", SWAP)
    in_a = lax.ppermute(parts[0, 1], "zh", SWAP)
    in_b = lax.ppermute(parts[1, 0], "zl", SWAP)
    in_c = lax.ppermute(parts[1, 1], ("zl", "zh"), [(0, 3), (1, 2), (2, 1), (3, 0)])
    own_sum = parts[0, 0] + in_a
    other_sum = in_b + in_c
    summed = jnp.stack(
        [jnp.where(zl == 0, own_sum, other_sum), jnp.where(zl == 0, other_sum, own_sum)]
    )
    new_column = -(summed * row_mask)
    reduced = landed.reshape(4, 2, 8, 16, Q).sum(axis=(0, 2))
    return (new_column, square + reduced)


def solution(mesh):
    fine = Mesh(mesh.devices.reshape(SIZES), AXES)
    in_specs = (P(PROW, PCOL), P(None, PROW, PCOL), P(), P(), P())
    out_specs = (P(None, PROW, PCOL), P(None, PROW, PCOL))
    return jax.shard_map(local, mesh=fine, in_specs=in_specs, out_specs=out_specs, check_vma=False)
```

```python
import jax
import jax.numpy as jnp
import numpy as np
from jax import lax
from jax.experimental import pallas as pl
from jax.experimental.pallas import tpu as pltpu
from jax.sharding import Mesh, PartitionSpec as P


W = 512
BS = 64
Q = 128
AXES = ("x", "zl", "y", "zh", "core")
SIZES = (4, 2, 4, 2, 2)
PROW = ("x", "zl", "y")
PCOL = ("zh", "core")

SWAP = [(0, 1), (1, 0)]
EVEN = [(0, 1), (1, 0), (2, 3), (3, 2)]
ODD = [(0, 3), (3, 0), (1, 2), (2, 1)]
ALL_VMEM = pl.BlockSpec(memory_space=pltpu.VMEM)


def route(where):
    pairs = []
    for source in np.ndindex(*SIZES):
        x, zl, y, zh, core = source
        target = where(x, zl, y, 2 * zh + core)
        tx, tzl, ty, tc = target
        pairs.append(
            (
                int(np.ravel_multi_index(source, SIZES)),
                int(np.ravel_multi_index((tx, tzl, ty, tc // 2, tc % 2), SIZES)),
            )
        )
    return pairs


def pick(x, i, dim):
    return lax.dynamic_index_in_dim(x, i, dim, keepdims=False)


def split(v):
    high = v.astype(jnp.bfloat16)
    return high, (v - high.astype(jnp.float32)).astype(jnp.bfloat16)


def dot3(left, right):
    ah, al = left
    bh, bl = right

    def one(a, b):
        return jnp.dot(a, b, preferred_element_type=jnp.float32)

    return one(ah, bh) + (one(ah, bl) + one(al, bh))


def position():
    return [lax.axis_index(name) for name in AXES]


def call(body, out_shape, arrays, limit, in_specs=None, scratch=()):
    return pl.pallas_call(
        body,
        out_shape=out_shape,
        in_specs=in_specs or [ALL_VMEM] * len(arrays),
        out_specs=(ALL_VMEM,) * len(out_shape),
        scratch_shapes=scratch,
        compiler_params=pltpu.CompilerParams(vmem_limit_bytes=limit * 1024 * 1024),
    )(*arrays)


def early(counts_hbm, ancestors_hbm, diag, square, col_mask, row_mask, out_mask, tile, counts, ancestors, sems):
    x, zl, y, zh, core = position()
    prow = 8 * x + 4 * zl + y
    pcol = 2 * zh + core
    fetch = [
        pltpu.make_async_copy(counts_hbm, counts, sems.at[0]),
        pltpu.make_async_copy(ancestors_hbm, ancestors, sems.at[1]),
    ]
    for copy in fetch:
        copy.start()
    for s in range(2):
        left = diag[s, :, pl.ds(pl.multiple_of((prow // 8) * Q, Q), Q)]
        right = diag[s, :, pl.ds(pl.multiple_of(pcol * Q, Q), Q)]
        tile[...] = dot3(split(left.T), split(right))
        square[s] = tile[pl.ds(pl.multiple_of((prow % 8) * 16, 16), 16), :]
    for copy in fetch:
        copy.wait()
    lane = lax.broadcasted_iota(jnp.int32, (32, 63), 1)
    slot = lax.broadcasted_iota(jnp.int32, (32, 63), 0)
    row_group = jnp.where(slot < 18, prow, prow + 4 - 8 * zl)
    block = jnp.where(slot < 16, (slot // 2) * 4 + pcol, row_group) + (slot % 2) * 32
    found = []
    for s in range(2):
        hit = (ancestors[s : s + 1, :] == block) & (lane < counts[s])
        found.append(jnp.max(hit.astype(jnp.float32), axis=1, keepdims=True))
        for j in range(2):
            out_mask[s, j * BS : (j + 1) * BS, :] = jnp.broadcast_to(found[s][16 + j : 17 + j, :], (BS, Q))
    owned = jnp.where(zl == 0, found[0], found[1])
    column = lax.broadcasted_iota(jnp.int32, (1, 8 * Q), 1) // BS
    mask = jnp.zeros((1, 8 * Q), jnp.float32)
    for j in range(16):
        mask = jnp.where(column == j, owned[j : j + 1, :], mask)
    col_mask[...] = mask
    for j in range(4):
        row_mask[j * BS : (j + 1) * BS, :] = jnp.broadcast_to(owned[16 + j : 17 + j, :], (BS, Q))


def left_factor(diag, row_mask, mine, g_zl, g_core, g_zh, hi_t, lo_t):
    _, zl, _, zh, core = position()
    pcol = 2 * zh + core
    quarters = (
        (mine[...], g_zl[...], pcol),
        (g_core[0], g_core[1], 2 * zh + 1 - core),
        (g_zh[0, 0], g_zh[0, 1], 2 - 2 * zh + core),
        (g_zh[1, 0], g_zh[1, 1], 3 - 2 * zh - core),
    )
    scaled = jnp.zeros((2 * Q, W), jnp.float32)
    for own, partner, quarter in quarters:
        rows = jnp.concatenate([own, partner], axis=0) * row_mask[...]
        start = pl.multiple_of(quarter * Q, Q)
        scaled = scaled + dot3(split(rows), split(diag[zl, pl.ds(start, Q), :]))
    hi, lo = split(scaled.T)
    hi_t[...] = hi
    lo_t[...] = lo


def products(
    band_own,
    band_other,
    col_mask,
    a1,
    a1r,
    a2,
    a2r,
    b1,
    b1r,
    b2,
    b2r,
    diag,
    part_keep,
    part_send,
    band_hi,
    band_lo,
    panel_hi,
    panel_lo,
    diag_hi,
    diag_lo,
):
    x, zl, y, zh, core = position()
    pieces = {}
    for ref, qs in ((a1, (0, 1)), (a1r, (3, 2))):
        for i, q in enumerate(qs):
            for j, xo in enumerate((0, 1)):
                pieces[0, xo, q] = (ref, i, j)
    for ref, qs in ((a2, (0, 3)), (a2r, (1, 2))):
        for i, q in enumerate(qs):
            for j, xo in enumerate((3, 2)):
                pieces[0, xo, q] = (ref, i, j)
    for ref, xs in ((b1, (0, 1)), (b1r, (3, 2))):
        for i, xo in enumerate(xs):
            for j, q in enumerate((0, 1)):
                pieces[1, xo, q] = (ref, i, j)
    for ref, xs in ((b2, (0, 3)), (b2r, (1, 2))):
        for i, xo in enumerate(xs):
            for j, q in enumerate((3, 2)):
                pieces[1, xo, q] = (ref, i, j)
    for (stream, xo, q), (ref, i, j) in pieces.items():
        hi, lo = split(ref[i, j])
        rows = slice((2 * xo + stream) * Q, (2 * xo + stream + 1) * Q)
        cols = slice(q * Q, (q + 1) * Q)
        panel_hi[rows, cols] = hi
        panel_lo[rows, cols] = lo
    for xo in range(4):
        for stream in range(2):
            side = zl if stream == 0 else 1 - zl
            start = pl.multiple_of((x ^ xo) * (2 * Q) + side * Q, Q)
            mask = col_mask[:, pl.ds(start, Q)]
            cols = slice((2 * xo + stream) * Q, (2 * xo + stream + 1) * Q)
            for r, ref in enumerate((band_own, band_other)):
                hi, lo = split(ref[:, pl.ds(start, Q)] * mask)
                band_hi[r * Q : (r + 1) * Q, cols] = hi
                band_lo[r * Q : (r + 1) * Q, cols] = lo
    for q in range(4):
        start = pl.multiple_of((y ^ q) * Q, Q)
        hi, lo = split(diag[zl, pl.ds(start, Q), :])
        diag_hi[q * Q : (q + 1) * Q, :] = hi
        diag_lo[q * Q : (q + 1) * Q, :] = lo
    product = dot3((band_hi[...], band_lo[...]), (panel_hi[...], panel_lo[...]))
    partial = dot3(split(product), (diag_hi[...], diag_lo[...]))
    for c in range(2):

        @pl.when(core == c)
        def _():
            for h in range(2):
                side = jnp.where(zh == h, 0, 1)
                for ref, k in ((part_keep, c), (part_send, 1 - c)):
                    part = partial[:, (2 * h + k) * Q : (2 * h + k + 1) * Q]
                    ref[:, side] = part.reshape(2, Q, Q)


def correction(part_keep, part_got, left_hi, left_lo, part, corr):
    _, _, _, zh, _ = position()
    part[...] = part_keep[...] + part_got[...]
    right = jnp.concatenate(
        [jnp.concatenate([part[0, s], part[1, s]], axis=0) for s in range(2)], axis=1
    )
    value = dot3((left_hi[...], left_lo[...]), split(right))
    corr[:, zh] = value[:, :Q].reshape(32, 16, Q)
    corr[:, 1 - zh] = value[:, Q:].reshape(32, 16, Q)


def f32(*shape):
    return jax.ShapeDtypeStruct(shape, jnp.float32)


def bf16(*shape):
    return jax.ShapeDtypeStruct(shape, jnp.bfloat16)


def vmem(*shapes):
    return [pltpu.VMEM(shape, jnp.bfloat16) for shape in shapes]


def step(band, panel, diag_inverse, ancestors, counts):
    zl = lax.axis_index("zl")
    mine = pick(panel, zl, 0)
    other = pick(panel, 1 - zl, 0)
    a_here = lax.ppermute(mine, AXES, route(lambda x, zl, y, c: (x, zl, c, y)))
    b_here = lax.ppermute(other, AXES, route(lambda x, zl, y, c: (x, 1 - zl, c, y)))
    band_other = lax.ppermute(band, "zl", SWAP)

    square, col_mask, row_mask, out_mask = call(
        early,
        (f32(2, 16, Q), f32(1, 8 * Q), f32(2 * Q, Q), f32(2, Q, Q)),
        (counts, ancestors, diag_inverse),
        12,
        in_specs=[pl.BlockSpec(memory_space=pl.ANY)] * 2 + [ALL_VMEM],
        scratch=[
            pltpu.VMEM((Q, Q), jnp.float32),
            pltpu.SMEM((2,), jnp.int32),
            pltpu.VMEM((2, 63), jnp.int32),
            pltpu.SemaphoreType.DMA((2,)),
        ],
    )
    a12 = jnp.stack([a_here, lax.ppermute(a_here, "x", EVEN)])
    b12 = jnp.stack([b_here, lax.ppermute(b_here, "y", EVEN)])
    a34 = lax.ppermute(a12, "x", ODD)
    b34 = lax.ppermute(b12, "y", ODD)
    a1 = jnp.stack([a12, lax.ppermute(a12, "y", EVEN)])
    b1 = jnp.stack([b12, lax.ppermute(b12, "x", EVEN)])
    a2 = jnp.stack([a34, lax.ppermute(a34, "y", ODD)])
    b2 = jnp.stack([b34, lax.ppermute(b34, "x", ODD)])
    a1r = lax.ppermute(a1, "y", ODD)
    b1r = lax.ppermute(b1, "x", ODD)
    a2r = lax.ppermute(a2, "y", EVEN)
    b2r = lax.ppermute(b2, "x", EVEN)

    g_zl = lax.ppermute(other, "zl", SWAP)
    rows = jnp.stack([mine, g_zl])
    g_core = lax.ppermute(rows, "core", SWAP)
    g_zh = lax.ppermute(jnp.stack([rows, g_core]), "zh", SWAP)
    left_hi, left_lo = call(
        left_factor,
        (bf16(W, 2 * Q), bf16(W, 2 * Q)),
        (diag_inverse, row_mask, mine, g_zl, g_core, g_zh),
        12,
    )
    part_keep, part_send = call(
        products,
        (f32(2, 2, Q, Q), f32(2, 2, Q, Q)),
        (band, band_other, col_mask, a1, a1r, a2, a2r, b1, b1r, b2, b2r, diag_inverse),
        20,
        scratch=vmem(*[(2 * Q, 8 * Q)] * 2, *[(8 * Q, W)] * 2, *[(W, W)] * 2),
    )
    part_got = lax.ppermute(part_send, "core", SWAP)
    parts, corr = call(
        correction,
        (f32(2, 2, Q, Q), f32(32, 2, 16, Q)),
        (part_keep, part_got, left_hi, left_lo),
        12,
    )
    landed = lax.all_to_all(corr.reshape(64, 16, Q), ("x", "zl", "y", "zh"), 0, 0, tiled=True)
    in_a = lax.ppermute(parts[0, 1], "zh", SWAP)
    in_b = lax.ppermute(parts[1, 0], "zl", SWAP)
    in_c = lax.ppermute(parts[1, 1], ("zl", "zh"), [(0, 3), (1, 2), (2, 1), (3, 0)])
    own_sum = parts[0, 0] + in_a
    other_sum = in_b + in_c
    summed = jnp.stack(
        [jnp.where(zl == 0, own_sum, other_sum), jnp.where(zl == 0, other_sum, own_sum)]
    )
    new_column = -(summed * out_mask)
    reduced = landed.reshape(4, 2, 8, 16, Q).sum(axis=(0, 2))
    return (new_column, square + reduced)


def solution(mesh):
    fine = Mesh(mesh.devices.reshape(SIZES), AXES)
    in_specs = (P(PROW, PCOL), P(None, PROW, PCOL), P(), P(), P())
    out_specs = (P(None, PROW, PCOL), P(None, PROW, PCOL))
    return jax.shard_map(step, mesh=fine, in_specs=in_specs, out_specs=out_specs, check_vma=False)
```

```python
import jax
import jax.numpy as jnp
import numpy as np
from jax import lax
from jax.experimental import pallas as pl
from jax.experimental.pallas import tpu as pltpu
from jax.sharding import Mesh, PartitionSpec as P


W = 512
BS = 64
Q = 128
AXES = ("x", "zl", "y", "zh", "core")
SIZES = (4, 2, 4, 2, 2)
PROW = ("x", "zl", "y")
PCOL = ("zh", "core")

SWAP = [(0, 1), (1, 0)]
EVEN = [(0, 1), (1, 0), (2, 3), (3, 2)]
FAR = [(0, 2), (2, 0), (1, 3), (3, 1)]
ODD = [(0, 3), (3, 0), (1, 2), (2, 1)]
ALL_VMEM = pl.BlockSpec(memory_space=pltpu.VMEM)


def route(where):
    pairs = []
    for source in np.ndindex(*SIZES):
        x, zl, y, zh, core = source
        target = where(x, zl, y, 2 * zh + core)
        tx, tzl, ty, tc = target
        pairs.append(
            (
                int(np.ravel_multi_index(source, SIZES)),
                int(np.ravel_multi_index((tx, tzl, ty, tc // 2, tc % 2), SIZES)),
            )
        )
    return pairs


def send(x, axes, pairs):
    return lax.ppermute(x, axes, pairs)


def pick(x, i, dim):
    return lax.dynamic_index_in_dim(x, i, dim, keepdims=False)


def split(v):
    high = v.astype(jnp.bfloat16)
    return high, (v - high.astype(jnp.float32)).astype(jnp.bfloat16)


def dot3(left, right):
    ah, al = left
    bh, bl = right

    def one(a, b):
        return jnp.dot(a, b, preferred_element_type=jnp.float32)

    return one(ah, bh) + (one(ah, bl) + one(al, bh))


def position():
    return [lax.axis_index(name) for name in AXES]


def call(body, out_shape, arrays, limit, in_specs=None, scratch=()):
    return pl.pallas_call(
        body,
        out_shape=out_shape,
        in_specs=in_specs or [ALL_VMEM] * len(arrays),
        out_specs=(ALL_VMEM,) * len(out_shape),
        scratch_shapes=scratch,
        compiler_params=pltpu.CompilerParams(vmem_limit_bytes=limit * 1024 * 1024),
    )(*arrays)


def early(
    counts_hbm,
    ancestors_hbm,
    diag_hbm,
    square,
    col_mask,
    row_mask,
    out_mask,
    diag_hi,
    diag_lo,
    tile,
    counts,
    ancestors,
    diag,
    sems,
):
    x, zl, y, zh, core = position()
    prow = 8 * x + 4 * zl + y
    pcol = 2 * zh + core
    fetch = [
        pltpu.make_async_copy(counts_hbm, counts, sems.at[0]),
        pltpu.make_async_copy(ancestors_hbm, ancestors, sems.at[1]),
        pltpu.make_async_copy(diag_hbm, diag, sems.at[2]),
    ]
    for copy in fetch:
        copy.start()
    for copy in fetch[:2]:
        copy.wait()
    lane = lax.broadcasted_iota(jnp.int32, (32, 63), 1)
    slot = lax.broadcasted_iota(jnp.int32, (32, 63), 0)
    row_group = jnp.where(slot < 18, prow, prow + 4 - 8 * zl)
    block = jnp.where(slot < 16, (slot // 2) * 4 + pcol, row_group) + (slot % 2) * 32
    found = []
    for s in range(2):
        hit = (ancestors[s : s + 1, :] == block) & (lane < counts[s])
        found.append(jnp.max(hit.astype(jnp.float32), axis=1, keepdims=True))
        for j in range(2):
            out_mask[s, j * BS : (j + 1) * BS, :] = jnp.broadcast_to(found[s][16 + j : 17 + j, :], (BS, Q))
    owned = jnp.where(zl == 0, found[0], found[1])
    column = lax.broadcasted_iota(jnp.int32, (1, 8 * Q), 1) // BS
    mask = jnp.zeros((1, 8 * Q), jnp.float32)
    for j in range(16):
        mask = jnp.where(column == j, owned[j : j + 1, :], mask)
    col_mask[...] = mask
    for j in range(4):
        row_mask[j * BS : (j + 1) * BS, :] = jnp.broadcast_to(owned[16 + j : 17 + j, :], (BS, Q))
    fetch[2].wait()
    for s in range(2):
        left = diag[s, :, pl.ds(pl.multiple_of((prow // 8) * Q, Q), Q)]
        right = diag[s, :, pl.ds(pl.multiple_of(pcol * Q, Q), Q)]
        tile[...] = dot3(split(left.T), split(right))
        square[s] = tile[pl.ds(pl.multiple_of((prow % 8) * 16, 16), 16), :]
    hi, lo = split(diag[zl])
    diag_hi[...] = hi
    diag_lo[...] = lo


def left_factor(diag_hi, diag_lo, row_mask, mine, g_zl, g_core, g_zh, hi_t, lo_t):
    _, _, _, zh, core = position()
    pcol = 2 * zh + core
    quarters = (
        (mine[...], g_zl[...], pcol),
        (g_core[0], g_core[1], 2 * zh + 1 - core),
        (g_zh[0, 0], g_zh[0, 1], 2 - 2 * zh + core),
        (g_zh[1, 0], g_zh[1, 1], 3 - 2 * zh - core),
    )
    scaled = jnp.zeros((2 * Q, W), jnp.float32)
    for own, partner, quarter in quarters:
        rows = jnp.concatenate([own, partner], axis=0) * row_mask[...]
        start = pl.multiple_of(quarter * Q, Q)
        scaled = scaled + dot3(split(rows), (diag_hi[pl.ds(start, Q), :], diag_lo[pl.ds(start, Q), :]))
    hi, lo = split(scaled.T)
    hi_t[...] = hi
    lo_t[...] = lo


def products(
    band_own,
    band_other,
    col_mask,
    a_all,
    a_even,
    a_far,
    a_odd,
    b_all,
    b_even,
    b_far,
    b_odd,
    diag_hi,
    diag_lo,
    part_keep,
    part_send,
    band_hi,
    band_lo,
    panel_hi,
    panel_lo,
    turned_hi,
    turned_lo,
):
    x, zl, y, zh, core = position()
    pieces = {}
    for outer, refs in enumerate(((a_all, a_even, a_far, a_odd), (b_all, b_even, b_far, b_odd))):
        for far, ref in enumerate(refs):
            for near in range(4):
                xo, q = (near, far) if outer == 0 else (far, near)
                pieces[outer, xo, q] = ref.at[near]
    for (stream, xo, q), ref in pieces.items():
        hi, lo = split(ref[...])
        rows = slice((2 * xo + stream) * Q, (2 * xo + stream + 1) * Q)
        cols = slice(q * Q, (q + 1) * Q)
        panel_hi[rows, cols] = hi
        panel_lo[rows, cols] = lo
    for xo in range(4):
        for stream in range(2):
            side = zl if stream == 0 else 1 - zl
            start = pl.multiple_of((x ^ xo) * (2 * Q) + side * Q, Q)
            mask = col_mask[:, pl.ds(start, Q)]
            cols = slice((2 * xo + stream) * Q, (2 * xo + stream + 1) * Q)
            for r, ref in enumerate((band_own, band_other)):
                hi, lo = split(ref[:, pl.ds(start, Q)] * mask)
                band_hi[r * Q : (r + 1) * Q, cols] = hi
                band_lo[r * Q : (r + 1) * Q, cols] = lo
    for q in range(4):
        start = pl.multiple_of((y ^ q) * Q, Q)
        turned_hi[q * Q : (q + 1) * Q, :] = diag_hi[pl.ds(start, Q), :]
        turned_lo[q * Q : (q + 1) * Q, :] = diag_lo[pl.ds(start, Q), :]
    product = dot3((band_hi[...], band_lo[...]), (panel_hi[...], panel_lo[...]))
    partial = dot3(split(product), (turned_hi[...], turned_lo[...]))
    for c in range(2):

        @pl.when(core == c)
        def _():
            for h in range(2):
                side = jnp.where(zh == h, 0, 1)
                for ref, k in ((part_keep, c), (part_send, 1 - c)):
                    part = partial[:, (2 * h + k) * Q : (2 * h + k + 1) * Q]
                    ref[:, side] = part.reshape(2, Q, Q)


def correction(part_keep, part_got, left_hi, left_lo, part, corr):
    _, _, _, zh, _ = position()
    part[...] = part_keep[...] + part_got[...]
    right = jnp.concatenate(
        [jnp.concatenate([part[0, s], part[1, s]], axis=0) for s in range(2)], axis=1
    )
    value = dot3((left_hi[...], left_lo[...]), split(right))
    corr[:, zh] = value[:, :Q].reshape(32, 16, Q)
    corr[:, 1 - zh] = value[:, Q:].reshape(32, 16, Q)


def finish(part, in_a, in_b, in_c, out_mask, landed, square, new_column, diag_block):
    _, zl, _, _, _ = position()
    new_column[zl] = -((part[...] + in_a[...]) * out_mask[zl])
    new_column[1 - zl] = -((in_b[...] + in_c[...]) * out_mask[1 - zl])
    for s in range(2):
        total = square[s]
        for i in range(4):
            for j in range(8):
                total = total + landed[i, s, j]
        diag_block[s] = total


def f32(*shape):
    return jax.ShapeDtypeStruct(shape, jnp.float32)


def bf16(*shape):
    return jax.ShapeDtypeStruct(shape, jnp.bfloat16)


def vmem(*shapes):
    return [pltpu.VMEM(shape, jnp.bfloat16) for shape in shapes]


def step(band, panel, diag_inverse, ancestors, counts):
    zl = lax.axis_index("zl")
    mine = pick(panel, zl, 0)
    other = pick(panel, 1 - zl, 0)
    a_here = send(mine, AXES, route(lambda x, zl, y, c: (x, zl, c, y)))
    b_here = send(other, AXES, route(lambda x, zl, y, c: (x, 1 - zl, c, y)))
    band_other = send(band, "zl", SWAP)

    square, col_mask, row_mask, out_mask, diag_hi, diag_lo = call(
        early,
        (f32(2, 16, Q), f32(1, 8 * Q), f32(2 * Q, Q), f32(2, Q, Q), bf16(W, W), bf16(W, W)),
        [pltpu.with_memory_space_constraint(v, pltpu.HBM) for v in (counts, ancestors, diag_inverse)],
        12,
        in_specs=[pl.BlockSpec(memory_space=pltpu.HBM)] * 3,
        scratch=[
            pltpu.VMEM((Q, Q), jnp.float32),
            pltpu.SMEM((2,), jnp.int32),
            pltpu.VMEM((2, 63), jnp.int32),
            pltpu.VMEM((2, W, W), jnp.float32),
            pltpu.SemaphoreType.DMA((3,)),
        ],
    )
    a4 = jnp.stack(
        [a_here, send(a_here, "x", EVEN), send(a_here, "x", FAR), send(a_here, "x", ODD)]
    )
    b4 = jnp.stack(
        [b_here, send(b_here, "y", EVEN), send(b_here, "y", FAR), send(b_here, "y", ODD)]
    )
    a_even, b_even = send(a4, "y", EVEN), send(b4, "x", EVEN)
    a_far, b_far = send(a4, "y", FAR), send(b4, "x", FAR)
    a_odd, b_odd = send(a4, "y", ODD), send(b4, "x", ODD)

    g_zl = send(other, "zl", SWAP)
    rows = jnp.stack([mine, g_zl])
    g_core = send(rows, "core", SWAP)
    g_zh = send(jnp.stack([rows, g_core]), "zh", SWAP)
    left_hi, left_lo = call(
        left_factor,
        (bf16(W, 2 * Q), bf16(W, 2 * Q)),
        (diag_hi, diag_lo, row_mask, mine, g_zl, g_core, g_zh),
        12,
    )
    part_keep, part_send = call(
        products,
        (f32(2, 2, Q, Q), f32(2, 2, Q, Q)),
        (
            (band, band_other, col_mask)
            + (a4, a_even, a_far, a_odd)
            + (b4, b_even, b_far, b_odd)
            + (diag_hi, diag_lo)
        ),
        20,
        scratch=vmem(*[(2 * Q, 8 * Q)] * 2, *[(8 * Q, W)] * 2, *[(W, W)] * 2),
    )
    part_got = send(part_send, "core", SWAP)
    parts, corr = call(
        correction,
        (f32(2, 2, Q, Q), f32(32, 2, 16, Q)),
        (part_keep, part_got, left_hi, left_lo),
        12,
    )
    landed = lax.all_to_all(corr.reshape(64, 16, Q), ("x", "zl", "y", "zh"), 0, 0, tiled=True)
    in_a = send(parts[0, 1], "zh", SWAP)
    in_b = send(parts[1, 0], "zl", SWAP)
    in_c = send(parts[1, 1], ("zl", "zh"), [(0, 3), (1, 2), (2, 1), (3, 0)])
    return call(
        finish,
        (f32(2, Q, Q), f32(2, 16, Q)),
        (parts[0, 0], in_a, in_b, in_c, out_mask, landed.reshape(4, 2, 8, 16, Q), square),
        12,
    )


def solution(mesh):
    fine = Mesh(mesh.devices.reshape(SIZES), AXES)
    in_specs = (P(PROW, PCOL), P(None, PROW, PCOL), P(), P(), P())
    out_specs = (P(None, PROW, PCOL), P(None, PROW, PCOL))
    return jax.shard_map(step, mesh=fine, in_specs=in_specs, out_specs=out_specs, check_vma=False)
```

```python
import jax
import jax.numpy as jnp
import numpy as np
from jax import lax
from jax.experimental import pallas as pl
from jax.experimental.pallas import tpu as pltpu
from jax.sharding import Mesh, PartitionSpec as P


W = 512
BS = 64
Q = 128
AXES = ("x", "zl", "y", "zh", "core")
SIZES = (4, 2, 4, 2, 2)
PROW = ("x", "zl", "y")
PCOL = ("zh", "core")

SWAP = [(0, 1), (1, 0)]
EVEN = [(0, 1), (1, 0), (2, 3), (3, 2)]
FAR = [(0, 2), (2, 0), (1, 3), (3, 1)]
ODD = [(0, 3), (3, 0), (1, 2), (2, 1)]
ALL_VMEM = pl.BlockSpec(memory_space=pltpu.VMEM)


def route(where):
    pairs = []
    for source in np.ndindex(*SIZES):
        x, zl, y, zh, core = source
        target = where(x, zl, y, 2 * zh + core)
        tx, tzl, ty, tc = target
        pairs.append(
            (
                int(np.ravel_multi_index(source, SIZES)),
                int(np.ravel_multi_index((tx, tzl, ty, tc // 2, tc % 2), SIZES)),
            )
        )
    return pairs


def send(x, axes, pairs):
    return lax.ppermute(x, axes, pairs)


def pick(x, i, dim):
    return lax.dynamic_index_in_dim(x, i, dim, keepdims=False)


def split(v):
    high = v.astype(jnp.bfloat16)
    return high, (v - high.astype(jnp.float32)).astype(jnp.bfloat16)


def dot3(left, right):
    ah, al = left
    bh, bl = right

    def one(a, b):
        return jnp.dot(a, b, preferred_element_type=jnp.float32)

    return one(ah, bh) + (one(ah, bl) + one(al, bh))


def position():
    return [lax.axis_index(name) for name in AXES]


def call(body, out_shape, arrays, limit, in_specs=None, scratch=()):
    return pl.pallas_call(
        body,
        out_shape=out_shape,
        in_specs=in_specs or [ALL_VMEM] * len(arrays),
        out_specs=(ALL_VMEM,) * len(out_shape),
        scratch_shapes=scratch,
        compiler_params=pltpu.CompilerParams(vmem_limit_bytes=limit * 1024 * 1024),
    )(*arrays)


def early(
    counts_hbm,
    ancestors_hbm,
    diag_hbm,
    mine,
    g_zl,
    g_core,
    band_own,
    band_other,
    square,
    col_mask,
    row_mask,
    out_mask,
    diag_hi,
    diag_lo,
    scaled,
    band_hi,
    band_lo,
    tile,
    counts,
    ancestors,
    diag,
    sems,
):
    x, zl, y, zh, core = position()
    prow = 8 * x + 4 * zl + y
    pcol = 2 * zh + core
    fetch = [
        pltpu.make_async_copy(counts_hbm, counts, sems.at[0]),
        pltpu.make_async_copy(ancestors_hbm, ancestors, sems.at[1]),
        pltpu.make_async_copy(diag_hbm, diag, sems.at[2]),
    ]
    for copy in fetch:
        copy.start()
    for copy in fetch[:2]:
        copy.wait()
    lane = lax.broadcasted_iota(jnp.int32, (32, 63), 1)
    slot = lax.broadcasted_iota(jnp.int32, (32, 63), 0)
    row_group = jnp.where(slot < 18, prow, prow + 4 - 8 * zl)
    block = jnp.where(slot < 16, (slot // 2) * 4 + pcol, row_group) + (slot % 2) * 32
    found = []
    for s in range(2):
        hit = (ancestors[s : s + 1, :] == block) & (lane < counts[s])
        found.append(jnp.max(hit.astype(jnp.float32), axis=1, keepdims=True))
        for j in range(2):
            out_mask[s, j * BS : (j + 1) * BS, :] = jnp.broadcast_to(found[s][16 + j : 17 + j, :], (BS, Q))
    owned = jnp.where(zl == 0, found[0], found[1])
    column = lax.broadcasted_iota(jnp.int32, (1, 8 * Q), 1) // BS
    mask = jnp.zeros((1, 8 * Q), jnp.float32)
    for j in range(16):
        mask = jnp.where(column == j, owned[j : j + 1, :], mask)
    col_mask[...] = mask
    for j in range(4):
        row_mask[j * BS : (j + 1) * BS, :] = jnp.broadcast_to(owned[16 + j : 17 + j, :], (BS, Q))
    fetch[2].wait()
    for s in range(2):
        left = diag[s, :, pl.ds(pl.multiple_of((prow // 8) * Q, Q), Q)]
        right = diag[s, :, pl.ds(pl.multiple_of(pcol * Q, Q), Q)]
        tile[...] = dot3(split(left.T), split(right))
        square[s] = tile[pl.ds(pl.multiple_of((prow % 8) * 16, 16), 16), :]
    hi, lo = split(diag[zl])
    diag_hi[...] = hi
    diag_lo[...] = lo
    quarters = ((mine[...], g_zl[...], pcol), (g_core[0], g_core[1], 2 * zh + 1 - core))
    scaled[...] = scaled_by(diag_hi, diag_lo, quarters)
    for xo in range(4):
        for stream in range(2):
            side = zl if stream == 0 else 1 - zl
            start = pl.multiple_of((x ^ xo) * (2 * Q) + side * Q, Q)
            mask = col_mask[:, pl.ds(start, Q)]
            cols = slice((2 * xo + stream) * Q, (2 * xo + stream + 1) * Q)
            for r, ref in enumerate((band_own, band_other)):
                hi, lo = split(ref[:, pl.ds(start, Q)] * mask)
                band_hi[r * Q : (r + 1) * Q, cols] = hi
                band_lo[r * Q : (r + 1) * Q, cols] = lo


def scaled_by(diag_hi, diag_lo, quarters):
    total = jnp.zeros((2 * Q, W), jnp.float32)
    for own, partner, quarter in quarters:
        rows = jnp.concatenate([own, partner], axis=0)
        start = pl.multiple_of(quarter * Q, Q)
        total = total + dot3(split(rows), (diag_hi[pl.ds(start, Q), :], diag_lo[pl.ds(start, Q), :]))
    return total


def left_factor(diag_hi, diag_lo, row_mask, scaled, g_zh, hi_t, lo_t):
    _, _, _, zh, core = position()
    quarters = (
        (g_zh[0, 0], g_zh[0, 1], 2 - 2 * zh + core),
        (g_zh[1, 0], g_zh[1, 1], 3 - 2 * zh - core),
    )
    total = (scaled[...] + scaled_by(diag_hi, diag_lo, quarters)) * row_mask[:, :1]
    hi, lo = split(total.T)
    hi_t[...] = hi
    lo_t[...] = lo


def gather_dot(band_hi, band_lo, blocks, xs, stream):
    slots = [slice((2 * xo + stream) * Q, (2 * xo + stream + 1) * Q) for xo in xs]
    left = [jnp.concatenate([ref[:, slot] for slot in slots], axis=1) for ref in (band_hi, band_lo)]
    return dot3(left, split(blocks))


def near_products(band_hi, band_lo, a_all, a_even, a_odd, b_all, b_even, b_odd, near):
    blocks = jnp.concatenate([ref[...].reshape(4 * Q, Q) for ref in (a_all, a_even, a_odd)], axis=1)
    first = gather_dot(band_hi, band_lo, blocks, range(4), 0)
    rows = [
        jnp.concatenate([ref[k] for k in range(4)], axis=1) for ref in (b_all, b_even, b_odd)
    ]
    second = gather_dot(band_hi, band_lo, jnp.concatenate(rows, axis=0), (0, 1, 3), 1)
    near[:, : 2 * Q] = first[:, : 2 * Q] + second[:, : 2 * Q]
    near[:, 2 * Q : 3 * Q] = second[:, 2 * Q : 3 * Q]
    near[:, 3 * Q :] = first[:, 2 * Q :] + second[:, 3 * Q :]


def products(
    band_hi, band_lo, near, a_far, b_far, diag_hi, diag_lo, part_keep, part_send, turned_hi, turned_lo, total
):
    _, _, y, zh, core = position()
    row = jnp.concatenate([b_far[k] for k in range(4)], axis=1)
    total[...] = near[...] + gather_dot(band_hi, band_lo, row, (2,), 1)
    column = a_far[...].reshape(4 * Q, Q)
    total[:, 2 * Q : 3 * Q] += gather_dot(band_hi, band_lo, column, range(4), 0)
    for q in range(4):
        start = pl.multiple_of((y ^ q) * Q, Q)
        turned_hi[q * Q : (q + 1) * Q, :] = diag_hi[pl.ds(start, Q), :]
        turned_lo[q * Q : (q + 1) * Q, :] = diag_lo[pl.ds(start, Q), :]
    product = total[...]
    partial = dot3(split(product), (turned_hi[...], turned_lo[...]))
    for c in range(2):

        @pl.when(core == c)
        def _():
            for h in range(2):
                side = jnp.where(zh == h, 0, 1)
                for ref, k in ((part_keep, c), (part_send, 1 - c)):
                    part = partial[:, (2 * h + k) * Q : (2 * h + k + 1) * Q]
                    ref[:, side] = part.reshape(2, Q, Q)


def correction(part_keep, part_got, left_hi, left_lo, part, corr):
    _, _, _, zh, _ = position()
    part[...] = part_keep[...] + part_got[...]
    right = jnp.concatenate(
        [jnp.concatenate([part[0, s], part[1, s]], axis=0) for s in range(2)], axis=1
    )
    value = dot3((left_hi[...], left_lo[...]), split(right))
    corr[:, zh] = value[:, :Q].reshape(32, 16, Q)
    corr[:, 1 - zh] = value[:, Q:].reshape(32, 16, Q)


def finish(part, in_a, in_b, in_c, out_mask, landed, square, new_column, diag_block):
    _, zl, _, _, _ = position()
    new_column[zl] = -((part[...] + in_a[...]) * out_mask[zl])
    new_column[1 - zl] = -((in_b[...] + in_c[...]) * out_mask[1 - zl])
    for s in range(2):
        total = square[s]
        for i in range(4):
            for j in range(8):
                total = total + landed[i, s, j]
        diag_block[s] = total


def f32(*shape):
    return jax.ShapeDtypeStruct(shape, jnp.float32)


def bf16(*shape):
    return jax.ShapeDtypeStruct(shape, jnp.bfloat16)


def vmem(*shapes):
    return [pltpu.VMEM(shape, jnp.bfloat16) for shape in shapes]


def step(band, panel, diag_inverse, ancestors, counts):
    zl = lax.axis_index("zl")
    mine = pick(panel, zl, 0)
    other = pick(panel, 1 - zl, 0)
    a_here = send(mine, AXES, route(lambda x, zl, y, c: (x, zl, c, y)))
    b_here = send(other, AXES, route(lambda x, zl, y, c: (x, 1 - zl, c, y)))
    band_other = send(band, "zl", SWAP)

    a4 = jnp.stack([a_here, send(a_here, "x", EVEN), send(a_here, "x", FAR), send(a_here, "x", ODD)])
    b4 = jnp.stack([b_here, send(b_here, "y", EVEN), send(b_here, "y", FAR), send(b_here, "y", ODD)])
    a_even, b_even = send(a4, "y", EVEN), send(b4, "x", EVEN)
    a_far, b_far = send(a4, "y", FAR), send(b4, "x", FAR)
    a_odd, b_odd = send(a4, "y", ODD), send(b4, "x", ODD)

    g_zl = send(other, "zl", SWAP)
    rows = jnp.stack([mine, g_zl])
    g_core = send(rows, "core", SWAP)
    g_zh = send(jnp.stack([rows, g_core]), "zh", SWAP)
    square, _, row_mask, out_mask, diag_hi, diag_lo, scaled, band_hi, band_lo = call(
        early,
        (f32(2, 16, Q), f32(1, 8 * Q), f32(2 * Q, Q), f32(2, Q, Q), bf16(W, W), bf16(W, W), f32(2 * Q, W))
        + (bf16(2 * Q, 8 * Q), bf16(2 * Q, 8 * Q)),
        [pltpu.with_memory_space_constraint(v, pltpu.HBM) for v in (counts, ancestors, diag_inverse)]
        + [mine, g_zl, g_core, band, band_other],
        12,
        in_specs=[pl.BlockSpec(memory_space=pltpu.HBM)] * 3 + [ALL_VMEM] * 5,
        scratch=[
            pltpu.VMEM((Q, Q), jnp.float32),
            pltpu.SMEM((2,), jnp.int32),
            pltpu.VMEM((2, 63), jnp.int32),
            pltpu.VMEM((2, W, W), jnp.float32),
            pltpu.SemaphoreType.DMA((3,)),
        ],
    )
    left_hi, left_lo = call(
        left_factor, (bf16(W, 2 * Q), bf16(W, 2 * Q)), (diag_hi, diag_lo, row_mask, scaled, g_zh), 12
    )
    (near,) = call(near_products, (f32(2 * Q, W),), (band_hi, band_lo, a4, a_even, a_odd, b4, b_even, b_odd), 16)
    part_keep, part_send = call(
        products,
        (f32(2, 2, Q, Q), f32(2, 2, Q, Q)),
        (band_hi, band_lo, near, a_far, b_far, diag_hi, diag_lo),
        16,
        scratch=vmem(*[(W, W)] * 2) + [pltpu.VMEM((2 * Q, W), jnp.float32)],
    )
    part_got = send(part_send, "core", SWAP)
    parts, corr = call(correction, (f32(2, 2, Q, Q), f32(32, 2, 16, Q)), (part_keep, part_got, left_hi, left_lo), 12)
    landed = lax.all_to_all(corr.reshape(64, 16, Q), ("x", "zl", "y", "zh"), 0, 0, tiled=True)
    in_a = send(parts[0, 1], "zh", SWAP)
    in_b = send(parts[1, 0], "zl", SWAP)
    in_c = send(parts[1, 1], ("zl", "zh"), [(0, 3), (1, 2), (2, 1), (3, 0)])
    return call(
        finish,
        (f32(2, Q, Q), f32(2, 16, Q)),
        (parts[0, 0], in_a, in_b, in_c, out_mask, landed.reshape(4, 2, 8, 16, Q), square),
        12,
    )


def solution(mesh):
    fine = Mesh(mesh.devices.reshape(SIZES), AXES)
    in_specs = (P(PROW, PCOL), P(None, PROW, PCOL), P(), P(), P())
    out_specs = (P(None, PROW, PCOL), P(None, PROW, PCOL))
    return jax.shard_map(step, mesh=fine, in_specs=in_specs, out_specs=out_specs, check_vma=False)
```

```python
import jax
import jax.numpy as jnp
import numpy as np
from jax import lax
from jax.experimental import pallas as pl
from jax.experimental.pallas import tpu as pltpu
from jax.sharding import Mesh, PartitionSpec as P


W = 512
BS = 64
Q = 128
AXES = ("x", "zl", "y", "zh", "core")
SIZES = (4, 2, 4, 2, 2)
PROW = ("x", "zl", "y")
PCOL = ("zh", "core")

SWAP = [(0, 1), (1, 0)]
EVEN = [(0, 1), (1, 0), (2, 3), (3, 2)]
FAR = [(0, 2), (2, 0), (1, 3), (3, 1)]
ODD = [(0, 3), (3, 0), (1, 2), (2, 1)]
ALL_VMEM = pl.BlockSpec(memory_space=pltpu.VMEM)


def route(where):
    pairs = []
    for source in np.ndindex(*SIZES):
        x, zl, y, zh, core = source
        target = where(x, zl, y, 2 * zh + core)
        tx, tzl, ty, tc = target
        pairs.append(
            (
                int(np.ravel_multi_index(source, SIZES)),
                int(np.ravel_multi_index((tx, tzl, ty, tc // 2, tc % 2), SIZES)),
            )
        )
    return pairs


def send(x, axes, pairs):
    return lax.ppermute(x, axes, pairs)


def pick(x, i, dim):
    return lax.dynamic_index_in_dim(x, i, dim, keepdims=False)


def split(v):
    high = v.astype(jnp.bfloat16)
    return high, (v - high.astype(jnp.float32)).astype(jnp.bfloat16)


def dot3(left, right):
    ah, al = left
    bh, bl = right

    def one(a, b):
        return jnp.dot(a, b, preferred_element_type=jnp.float32)

    return one(ah, bh) + (one(ah, bl) + one(al, bh))


def position():
    return [lax.axis_index(name) for name in AXES]


def call(body, out_shape, arrays, limit, in_specs=None, scratch=()):
    return pl.pallas_call(
        body,
        out_shape=out_shape,
        in_specs=in_specs or [ALL_VMEM] * len(arrays),
        out_specs=(ALL_VMEM,) * len(out_shape),
        scratch_shapes=scratch,
        compiler_params=pltpu.CompilerParams(vmem_limit_bytes=limit * 1024 * 1024),
    )(*arrays)


def early(
    counts_hbm,
    ancestors_hbm,
    diag_hbm,
    mine,
    g_zl,
    g_core,
    band_own,
    band_other,
    square,
    col_mask,
    row_mask,
    out_mask,
    diag_hi,
    diag_lo,
    scaled,
    band_hi,
    band_lo,
    tile,
    counts,
    ancestors,
    diag,
    sems,
):
    x, zl, y, zh, core = position()
    prow = 8 * x + 4 * zl + y
    pcol = 2 * zh + core
    fetch = [
        pltpu.make_async_copy(counts_hbm, counts, sems.at[0]),
        pltpu.make_async_copy(ancestors_hbm, ancestors, sems.at[1]),
        pltpu.make_async_copy(diag_hbm, diag, sems.at[2]),
    ]
    for copy in fetch:
        copy.start()
    for copy in fetch[:2]:
        copy.wait()
    lane = lax.broadcasted_iota(jnp.int32, (32, 63), 1)
    slot = lax.broadcasted_iota(jnp.int32, (32, 63), 0)
    row_group = jnp.where(slot < 18, prow, prow + 4 - 8 * zl)
    block = jnp.where(slot < 16, (slot // 2) * 4 + pcol, row_group) + (slot % 2) * 32
    found = []
    for s in range(2):
        hit = (ancestors[s : s + 1, :] == block) & (lane < counts[s])
        found.append(jnp.max(hit.astype(jnp.float32), axis=1, keepdims=True))
        for j in range(2):
            out_mask[s, j * BS : (j + 1) * BS, :] = jnp.broadcast_to(found[s][16 + j : 17 + j, :], (BS, Q))
    owned = jnp.where(zl == 0, found[0], found[1])
    column = lax.broadcasted_iota(jnp.int32, (1, 8 * Q), 1) // BS
    mask = jnp.zeros((1, 8 * Q), jnp.float32)
    for j in range(16):
        mask = jnp.where(column == j, owned[j : j + 1, :], mask)
    col_mask[...] = mask
    for j in range(4):
        row_mask[j * BS : (j + 1) * BS, :] = jnp.broadcast_to(owned[16 + j : 17 + j, :], (BS, Q))
    fetch[2].wait()
    for s in range(2):
        left = diag[s, :, pl.ds(pl.multiple_of((prow // 8) * Q, Q), Q)]
        right = diag[s, :, pl.ds(pl.multiple_of(pcol * Q, Q), Q)]
        tile[...] = dot3(split(left.T), split(right))
        square[s] = tile[pl.ds(pl.multiple_of((prow % 8) * 16, 16), 16), :]
    hi, lo = split(diag[zl])
    diag_hi[...] = hi
    diag_lo[...] = lo
    quarters = ((mine[...], g_zl[...], pcol), (g_core[0], g_core[1], 2 * zh + 1 - core))
    scaled[...] = scaled_by(diag_hi, diag_lo, quarters)
    for xo in range(4):
        for stream in range(2):
            side = zl if stream == 0 else 1 - zl
            start = pl.multiple_of((x ^ xo) * (2 * Q) + side * Q, Q)
            mask = col_mask[:, pl.ds(start, Q)]
            cols = slice((2 * xo + stream) * Q, (2 * xo + stream + 1) * Q)
            for r, ref in enumerate((band_own, band_other)):
                hi, lo = split(ref[:, pl.ds(start, Q)] * mask)
                band_hi[r * Q : (r + 1) * Q, cols] = hi
                band_lo[r * Q : (r + 1) * Q, cols] = lo


def scaled_by(diag_hi, diag_lo, quarters):
    total = jnp.zeros((2 * Q, W), jnp.float32)
    for own, partner, quarter in quarters:
        rows = jnp.concatenate([own, partner], axis=0)
        start = pl.multiple_of(quarter * Q, Q)
        total = total + dot3(split(rows), (diag_hi[pl.ds(start, Q), :], diag_lo[pl.ds(start, Q), :]))
    return total


def left_factor(diag_hi, diag_lo, row_mask, scaled, g_zh, hi_t, lo_t):
    _, _, _, zh, core = position()
    quarters = (
        (g_zh[0, 0], g_zh[0, 1], 2 - 2 * zh + core),
        (g_zh[1, 0], g_zh[1, 1], 3 - 2 * zh - core),
    )
    total = (scaled[...] + scaled_by(diag_hi, diag_lo, quarters)) * row_mask[:, :1]
    hi, lo = split(total.T)
    hi_t[...] = hi
    lo_t[...] = lo


def products(
    band_hi,
    band_lo,
    a_all,
    a_even,
    a_far,
    a_odd,
    b_all,
    b_even,
    b_far,
    b_odd,
    diag_hi,
    diag_lo,
    part_keep,
    part_send,
    panel_hi,
    panel_lo,
    turned_hi,
    turned_lo,
):
    _, _, y, zh, core = position()
    pieces = {}
    for outer, refs in enumerate(((a_all, a_even, a_far, a_odd), (b_all, b_even, b_far, b_odd))):
        for far, ref in enumerate(refs):
            for near in range(4):
                xo, q = (near, far) if outer == 0 else (far, near)
                pieces[outer, xo, q] = ref.at[near]
    for (stream, xo, q), ref in pieces.items():
        hi, lo = split(ref[...])
        rows = slice((2 * xo + stream) * Q, (2 * xo + stream + 1) * Q)
        cols = slice(q * Q, (q + 1) * Q)
        panel_hi[rows, cols] = hi
        panel_lo[rows, cols] = lo
    for q in range(4):
        start = pl.multiple_of((y ^ q) * Q, Q)
        turned_hi[q * Q : (q + 1) * Q, :] = diag_hi[pl.ds(start, Q), :]
        turned_lo[q * Q : (q + 1) * Q, :] = diag_lo[pl.ds(start, Q), :]
    product = dot3((band_hi[...], band_lo[...]), (panel_hi[...], panel_lo[...]))
    partial = dot3(split(product), (turned_hi[...], turned_lo[...]))
    for c in range(2):

        @pl.when(core == c)
        def _():
            for h in range(2):
                side = jnp.where(zh == h, 0, 1)
                for ref, k in ((part_keep, c), (part_send, 1 - c)):
                    part = partial[:, (2 * h + k) * Q : (2 * h + k + 1) * Q]
                    ref[:, side] = part.reshape(2, Q, Q)


def correction(part_keep, part_got, left_hi, left_lo, part, corr):
    _, _, _, zh, _ = position()
    part[...] = part_keep[...] + part_got[...]
    right = jnp.concatenate(
        [jnp.concatenate([part[0, s], part[1, s]], axis=0) for s in range(2)], axis=1
    )
    value = dot3((left_hi[...], left_lo[...]), split(right))
    corr[:, zh] = value[:, :Q].reshape(32, 16, Q)
    corr[:, 1 - zh] = value[:, Q:].reshape(32, 16, Q)


def finish(part, in_a, in_b, in_c, out_mask, landed, square, new_column, diag_block):
    _, zl, _, _, _ = position()
    new_column[zl] = -((part[...] + in_a[...]) * out_mask[zl])
    new_column[1 - zl] = -((in_b[...] + in_c[...]) * out_mask[1 - zl])
    for s in range(2):
        total = square[s]
        for i in range(4):
            for j in range(8):
                total = total + landed[i, s, j]
        diag_block[s] = total


def f32(*shape):
    return jax.ShapeDtypeStruct(shape, jnp.float32)


def bf16(*shape):
    return jax.ShapeDtypeStruct(shape, jnp.bfloat16)


def vmem(*shapes):
    return [pltpu.VMEM(shape, jnp.bfloat16) for shape in shapes]


def step(band, panel, diag_inverse, ancestors, counts):
    zl = lax.axis_index("zl")
    mine = pick(panel, zl, 0)
    other = pick(panel, 1 - zl, 0)
    a_here = send(mine, AXES, route(lambda x, zl, y, c: (x, zl, c, y)))
    b_here = send(other, AXES, route(lambda x, zl, y, c: (x, 1 - zl, c, y)))
    band_other = send(band, "zl", SWAP)

    a4 = jnp.stack(
        [a_here, send(a_here, "x", EVEN), send(a_here, "x", FAR), send(a_here, "x", ODD)]
    )
    b4 = jnp.stack(
        [b_here, send(b_here, "y", EVEN), send(b_here, "y", FAR), send(b_here, "y", ODD)]
    )
    a_even, b_even = send(a4, "y", EVEN), send(b4, "x", EVEN)
    a_far, b_far = send(a4, "y", FAR), send(b4, "x", FAR)
    a_odd, b_odd = send(a4, "y", ODD), send(b4, "x", ODD)

    g_zl = send(other, "zl", SWAP)
    rows = jnp.stack([mine, g_zl])
    g_core = send(rows, "core", SWAP)
    g_zh = send(jnp.stack([rows, g_core]), "zh", SWAP)
    square, _, row_mask, out_mask, diag_hi, diag_lo, scaled, band_hi, band_lo = call(
        early,
        (f32(2, 16, Q), f32(1, 8 * Q), f32(2 * Q, Q), f32(2, Q, Q), bf16(W, W), bf16(W, W), f32(2 * Q, W))
        + (bf16(2 * Q, 8 * Q), bf16(2 * Q, 8 * Q)),
        [pltpu.with_memory_space_constraint(v, pltpu.HBM) for v in (counts, ancestors, diag_inverse)]
        + [mine, g_zl, g_core, band, band_other],
        12,
        in_specs=[pl.BlockSpec(memory_space=pltpu.HBM)] * 3 + [ALL_VMEM] * 5,
        scratch=[
            pltpu.VMEM((Q, Q), jnp.float32),
            pltpu.SMEM((2,), jnp.int32),
            pltpu.VMEM((2, 63), jnp.int32),
            pltpu.VMEM((2, W, W), jnp.float32),
            pltpu.SemaphoreType.DMA((3,)),
        ],
    )
    left_hi, left_lo = call(
        left_factor,
        (bf16(W, 2 * Q), bf16(W, 2 * Q)),
        (diag_hi, diag_lo, row_mask, scaled, g_zh),
        12,
    )
    part_keep, part_send = call(
        products,
        (f32(2, 2, Q, Q), f32(2, 2, Q, Q)),
        (
            (band_hi, band_lo)
            + (a4, a_even, a_far, a_odd)
            + (b4, b_even, b_far, b_odd)
            + (diag_hi, diag_lo)
        ),
        20,
        scratch=vmem(*[(8 * Q, W)] * 2, *[(W, W)] * 2),
    )
    part_got = send(part_send, "core", SWAP)
    parts, corr = call(
        correction,
        (f32(2, 2, Q, Q), f32(32, 2, 16, Q)),
        (part_keep, part_got, left_hi, left_lo),
        12,
    )
    landed = lax.all_to_all(corr.reshape(64, 16, Q), ("x", "zl", "y", "zh"), 0, 0, tiled=True)
    in_a = send(parts[0, 1], "zh", SWAP)
    in_b = send(parts[1, 0], "zl", SWAP)
    in_c = send(parts[1, 1], ("zl", "zh"), [(0, 3), (1, 2), (2, 1), (3, 0)])
    return call(
        finish,
        (f32(2, Q, Q), f32(2, 16, Q)),
        (parts[0, 0], in_a, in_b, in_c, out_mask, landed.reshape(4, 2, 8, 16, Q), square),
        12,
    )


def solution(mesh):
    fine = Mesh(mesh.devices.reshape(SIZES), AXES)
    in_specs = (P(PROW, PCOL), P(None, PROW, PCOL), P(), P(), P())
    out_specs = (P(None, PROW, PCOL), P(None, PROW, PCOL))
    return jax.shard_map(step, mesh=fine, in_specs=in_specs, out_specs=out_specs, check_vma=False)
```
